32 devices in a mesh: dom: 16 (over z, x, core), band: 2 (over y).
Axes of the slice: x: 2, y: 2, z: 4, core: 2. Of those that a mesh axis runs over, the one named last changes fastest.
Arguments:
- wavefun: float32 [13824, 512], P('dom', 'band')
- cell_ops: float32 [64, 343, 343], P('dom'), as said below
- cell_map: int32 [64, 343], P('dom'), may hold values from 0 to 1007, as said below
- face_list: int32 [2304], P('dom'), may hold values from 0 to 863, as said below
Outputs:
- ortho_bands: float32 [13824, 512], P('dom', 'band')
The draws below stay inside these ranges and needn't reach their ends.
Inputs may be any that keep to these rules, and one draw needn't show every extreme that they name: `cell_map`: each row lists the 343 distinct local numbers of a cell's nodes; a number below 864 is a node of the cell's own domain, 864 + j stands for the j-th lower face node of the next domain (periodic over domains); every node of a domain belongs to some cell of that domain. `face_list`: the 144 entries of each domain are distinct node numbers of that domain. `cell_ops`: each cell's matrix is symmetric.
All inputs are finite; a program needn't handle non-finite values.
Results may differ from the reference program's by a relative error of at most 0.0001.
Values sent between devices are 32-bit elements; how exact they have to be, the bound alone decides.
A program may use at most 64 MiB of HBM per device.

```python
import math
import jax
import jax.numpy as jnp
from jax import lax

P_SIZE = 6
LX = 1
NB = 512
DEGREE = 2
NODE_CELL = 343
FACE = 144
OWN = 864
CELLS = 4
DOMAINS = 16
NODES = 13824
ALL_CELLS = 64


def geometry(key):
    geo_key = jax.random.fold_in(key, 11)
    side = 2 * P_SIZE
    layers = P_SIZE * LX
    per_side = P_SIZE + 1
    cell_index = jnp.arange(CELLS, dtype=jnp.int32)[:, None]
    node_index = jnp.arange(NODE_CELL, dtype=jnp.int32)[None, :]
    cell_x = cell_index // 4
    cell_y = cell_index // 2 % 2
    cell_z = cell_index % 2
    along_a = node_index // (per_side * per_side)
    along_b = node_index // per_side % per_side
    along_e = node_index % per_side
    pos_x = cell_x * P_SIZE + along_a
    pos_y = (cell_y * P_SIZE + along_b) % side
    pos_z = (cell_z * P_SIZE + along_e) % side
    geo_index = jnp.clip((pos_x * side + pos_y) * side + pos_z, 0, OWN - 1).reshape(-1)
    face_index = (pos_y * side + pos_z).reshape(-1)
    inside = (pos_x < layers).reshape(-1)
    domain_keys = jax.random.split(geo_key, DOMAINS)
    labels = jax.vmap(lambda one_key: jax.random.permutation(one_key, OWN).astype(jnp.int32))(domain_keys)
    mapped = jnp.where(inside[None, :], labels[:, geo_index], OWN + face_index[None, :])
    cell_table = mapped.reshape(ALL_CELLS, NODE_CELL).astype(jnp.int32)
    face_table = labels[:, :FACE].reshape(-1).astype(jnp.int32)
    return (cell_table, face_table)


def draw_cell_map(key, part):
    return geometry(key)[0]


def draw_face_list(key, part):
    return geometry(key)[1]


def draw_cell_ops(key, part):
    ops_key = jax.random.fold_in(key, 5)
    noise_key, diag_key = jax.random.split(ops_key)
    noise = jax.random.normal(noise_key, (ALL_CELLS, NODE_CELL, NODE_CELL), jnp.float32)
    symmetric = (noise + jnp.swapaxes(noise, 1, 2)) / math.sqrt(2.0) * (0.055 / math.sqrt(NODE_CELL))
    diagonal = jax.random.uniform(diag_key, (ALL_CELLS, NODE_CELL), jnp.float32, 0.05, 0.2)
    identity = jnp.eye(NODE_CELL, dtype=jnp.float32)
    return symmetric + diagonal[:, :, None] * identity[None, :, :]


def draw_wavefun(key, part):
    wave_key = jax.random.fold_in(key, 3)
    keys = jax.random.split(wave_key, 5)
    base = jax.random.normal(keys[0], (NODES, NB), jnp.float32)
    common_weight = 0.5
    column_scale = jnp.exp(jax.random.uniform(keys[1], (NB,), jnp.float32, math.log(0.5), math.log(5.0)))
    row_rand = jnp.exp(jax.random.uniform(keys[2], (NODES,), jnp.float32, math.log(0.3), math.log(3.0)))
    domain_pos = (jnp.arange(NODES, dtype=jnp.int32) // OWN).astype(jnp.float32)
    row_scale = row_rand * (1.0 + 2.0 * domain_pos / (DOMAINS - 1)) / 2.0
    common_left = jax.random.normal(keys[3], (NODES, 48), jnp.float32)
    common_right = jax.random.normal(keys[4], (48, NB), jnp.float32) / math.sqrt(48.0)
    common = jnp.dot(common_left, common_right)
    return row_scale[:, None] * (base * column_scale[None, :] + common_weight * common)


def setup_inputs(seed: int = 0) -> dict:
    key_of = jax.random.split(jax.random.key(seed), 5)
    return {
        "wavefun": draw_wavefun(jax.random.fold_in(key_of[4], 71), 0),
        "cell_ops": draw_cell_ops(jax.random.fold_in(key_of[4], 71), 0),
        "cell_map": draw_cell_map(jax.random.fold_in(key_of[4], 71), 0),
        "face_list": draw_face_list(jax.random.fold_in(key_of[4], 71), 0),
    }


cheb_centre = 1.0
cheb_half = 1.6

def reference(wavefun, cell_ops, cell_map, face_list):
    domain_of = jnp.arange(ALL_CELLS, dtype=jnp.int32) // CELLS
    next_domain = (domain_of + 1) % DOMAINS
    face_slot = jnp.clip(cell_map - OWN, 0, FACE - 1).astype(jnp.int32)
    neighbour_node = next_domain[:, None] * OWN + face_list[next_domain[:, None] * FACE + face_slot]
    global_node = jnp.where(cell_map < OWN, domain_of[:, None] * OWN + cell_map, neighbour_node).astype(jnp.int32)
    flat_nodes = global_node.reshape(-1)

    def operate(vector):

        def one_domain(domain_index):
            nodes = lax.dynamic_slice_in_dim(global_node, domain_index * CELLS, CELLS, 0)
            matrices = lax.dynamic_slice_in_dim(cell_ops, domain_index * CELLS, CELLS, 0)
            gathered = vector[nodes]
            return jnp.einsum('cij,cjb->cib', matrices, gathered, precision=lax.Precision.HIGHEST)
        products = lax.map(one_domain, jnp.arange(DOMAINS, dtype=jnp.int32))
        return jnp.zeros_like(vector).at[flat_nodes].add(products.reshape(-1, NB))
    earlier = wavefun
    latest = (operate(wavefun) - cheb_centre * wavefun) / cheb_half
    for counter in range(1, DEGREE):
        following = 2.0 * (operate(latest) - cheb_centre * latest) / cheb_half - earlier
        earlier = latest
        latest = following
    filtered = latest
    margin = jnp.einsum('nb,nc->bc', filtered, filtered, precision=lax.Precision.HIGHEST)
    norm_value = jnp.sqrt(jnp.sum(margin * margin) + 1e-06)
    scaled = margin / norm_value
    identity = jnp.eye(NB, dtype=jnp.float32)
    mixing = (3.0 * identity - scaled) / 2.0
    return jnp.dot(filtered, mixing, precision=lax.Precision.HIGHEST)
```

```python
import functools
import types

import jax
import jax.numpy as jnp
from jax import lax
from jax.experimental import pallas as pl
from jax.experimental.pallas import tpu as pltpu
from jax.sharding import PartitionSpec as P

DEGREE = 2


cheb_centre = 1.0
cheb_half = 1.6

f32 = jnp.float32
bf16 = jnp.bfloat16
MESH = pl.DeviceIdType.MESH


def round_up(value, step):
    return (value + step - 1) // step * step


def halves(value):
    high = value.astype(bf16)
    low = (value - high.astype(f32)).astype(bf16)
    return high, low


def dot(left, right):
    return jnp.dot(left, right, preferred_element_type=f32)


def dot_tn(left, right):
    return lax.dot_general(left, right, (((0,), (0,)), ((), ())), preferred_element_type=f32)


def dot_nt(left, right):
    return lax.dot_general(left, right, (((1,), (1,)), ((), ())), preferred_element_type=f32)


class Sizes:
    def __init__(self, n_dom, n_band, own, width, cells, nodes, face):
        self.n_dom, self.n_band = n_dom, n_band
        self.own, self.width = own, width
        self.cells, self.nodes, self.face = cells, nodes, face
        self.own_pad = round_up(own, 128)
        self.face_pad = round_up(face, 128)
        self.rows = round_up(nodes, 16)
        self.lanes = round_up(nodes, 128)
        self.half_pad = round_up(own // 2, 128)
        self.chips = n_dom // 2
        self.chunk = width // n_dom
        self.packet = self.chunk + 8
        self.gram = (
            n_band == 2
            and n_dom % 2 == 0
            and n_dom > 2
            and width % (8 * n_dom) == 0
            and width % 128 == 0
            and own % 32 == 0
        )


def start_all(copies):
    for copy in copies:
        copy.start()


def wait_all(copies):
    for copy in copies:
        copy.wait()


def filter_steps(s, ready, wave_ref, ops_ref, map_ref, face_ref, result_ref, w):
    me = lax.axis_index("dom")
    right = lax.rem(me + 1, s.n_dom)
    left = lax.rem(me + s.n_dom - 1, s.n_dom)
    C, R, L, W = s.cells, s.rows, s.lanes, s.width

    def split_store(ref, first, value):
        high, low = halves(value)
        ref[pl.ds(first, value.shape[0]), pl.ds(0, W)] = high
        ref[pl.ds(first, value.shape[0]), pl.ds(W, W)] = low

    def merged(wide):
        return wide[:, :W] + wide[:, W:]

    w.index[...] = jnp.full(w.index.shape, -1.0, f32)
    w.index[pl.ds(0, C), pl.ds(0, s.nodes)] = map_ref[...].astype(f32)
    w.index[pl.ds(C, 1), pl.ds(0, s.face)] = face_ref[...].astype(f32)
    columns = jnp.transpose(w.index[...])

    def one_hot(match):
        return jnp.where(match, 1.0, 0.0).astype(bf16)

    def iota(shape, axis):
        return lax.broadcasted_iota(jnp.int32, shape, axis).astype(f32)

    w.face_rows[...] = one_hot(columns[: s.face, C : C + 1] == iota((s.face, s.own_pad), 1))
    w.vec[pl.ds(s.own, s.own_pad - s.own), :] = jnp.zeros((s.own_pad - s.own, 2 * W), bf16)
    split_store(w.vec, 0, wave_ref[...])

    def face_copy(step):
        return pltpu.make_async_remote_copy(
            src_ref=w.face_send.at[step], dst_ref=w.face_recv.at[step],
            send_sem=w.face_ssem.at[step], recv_sem=w.face_rsem.at[step],
            device_id={"dom": left}, device_id_type=MESH)

    def back_copy(step):
        return pltpu.make_async_remote_copy(
            src_ref=w.back_send.at[step], dst_ref=w.back_recv.at[step],
            send_sem=w.back_ssem.at[step], recv_sem=w.back_rsem.at[step],
            device_id={"dom": right}, device_id_type=MESH)

    w.face_send[0] = merged(dot(w.face_rows[...], w.vec[...]))
    ready()
    face_copy(0).start()

    w.op_pad[...] = jnp.zeros(w.op_pad.shape, f32)
    for c in range(C):
        column = columns[:R, c : c + 1]
        w.take_own[c] = one_hot(column == iota((R, s.own_pad), 1))
        w.take_face[c] = one_hot(column - float(s.own) == iota((R, s.face_pad), 1))
        row = w.index[c : c + 1, :]
        w.put_own[:, pl.ds(c * L, L)] = one_hot(row == iota((s.own, L), 0))
        w.put_face[:, pl.ds(c * L, L)] = one_hot(row - float(s.own) == iota((s.face, L), 0))
        w.op_pad[c, pl.ds(0, s.nodes), pl.ds(0, s.nodes)] = ops_ref[c]
        high, low = halves(w.op_pad[c])
        w.op_high[c] = high
        w.op_low[c] = low
        if L > R:
            w.prod[pl.ds(c * L + R, L - R), :] = jnp.zeros((L - R, 2 * W), bf16)
            w.cell[c, pl.ds(R, L - R), :] = jnp.zeros((L - R, 2 * W), bf16)
    w.put_back[...] = one_hot(w.index[C : C + 1, pl.ds(0, s.face_pad)] == iota((s.own, s.face_pad), 0))
    if s.face_pad > s.face:
        w.far[pl.ds(s.face, s.face_pad - s.face), :] = jnp.zeros((s.face_pad - s.face, 2 * W), bf16)

    for step in range(DEGREE):
        if step > 0:
            split_store(w.vec, 0, w.latest[...])
            w.face_send[step] = merged(dot(w.face_rows[...], w.vec[...]))
            face_copy(step).start()
        for c in range(C):
            w.part[c] = dot(w.take_own[c], w.vec[...])
        face_copy(step).wait()
        split_store(w.far, 0, w.face_recv[step])
        for c in range(C):
            cell = w.part[c] + dot(w.take_face[c], w.far[...])
            w.cell[c, pl.ds(0, R), :] = cell.astype(bf16)
            wide = dot(w.op_high[c], w.cell[c])
            value = wide[:, :W] + wide[:, W:] + dot(w.op_low[c], w.cell[c, :, pl.ds(0, W)])
            split_store(w.prod, c * L, value)
        w.back_send[step] = merged(dot(w.put_face[...], w.prod[...]))
        back_copy(step).start()
        applied = merged(dot(w.put_own[...], w.prod[...]))
        back_copy(step).wait()
        split_store(w.far, 0, w.back_recv[step])
        applied = applied + merged(dot(w.put_back[...], w.far[...]))
        current = wave_ref[...] if step == 0 else w.latest[...]
        if step == 0:
            following = (applied - cheb_centre * current) / cheb_half
        else:
            earlier = wave_ref[...] if step == 1 else w.older[...]
            following = 2.0 * (applied - cheb_centre * current) / cheb_half - earlier
        if step == DEGREE - 1:
            result_ref[...] = following
        else:
            if step > 0 and step < DEGREE - 1:
                w.older[...] = current
            w.latest[...] = following


def gram_steps(s, band_ref, out_ref, w):
    me = lax.axis_index("dom")
    band = lax.axis_index("band")
    other = 1 - band
    chip, core = me // 2, lax.rem(me, 2)
    partner = chip * 2 + (1 - core)
    W, half, n, chunk = s.width, s.own // 2, s.chips, s.chunk

    def band_copy(turn, first):
        rows = pl.ds(pl.multiple_of(first * half, 8), half)
        return pltpu.make_async_remote_copy(
            src_ref=band_ref.at[rows, :], dst_ref=w.far_band.at[rows, :],
            send_sem=w.band_ssem.at[turn], recv_sem=w.band_rsem.at[turn],
            device_id={"band": other}, device_id_type=MESH)

    def core_copy(m):
        return pltpu.make_async_remote_copy(
            src_ref=w.sums.at[m, 1 - core], dst_ref=w.core_recv.at[m],
            send_sem=w.core_ssem.at[m], recv_sem=w.core_rsem.at[m],
            device_id={"dom": partner}, device_id_type=MESH)

    def scatter_copies(m):
        copies = []
        for j in range(1, n):
            target = lax.rem(chip + j, n)
            copies.append(pltpu.make_async_remote_copy(
                src_ref=w.pair.at[m, target], dst_ref=w.scat_recv.at[m, j - 1],
                send_sem=w.scat_ssem.at[m, j - 1], recv_sem=w.scat_rsem.at[m, j - 1],
                device_id={"dom": target * 2 + core}, device_id_type=MESH))
        return copies

    def gather_copies(m):
        copies = []
        for j in range(1, n):
            target = lax.rem(chip + j, n)
            copies.append(pltpu.make_async_remote_copy(
                src_ref=w.full.at[m, core, chip], dst_ref=w.full.at[m, core, chip],
                send_sem=w.gath_ssem.at[m, j - 1], recv_sem=w.gath_rsem.at[m, j - 1],
                device_id={"dom": target * 2 + core}, device_id_type=MESH))
        return copies

    def swap_copy(m):
        return pltpu.make_async_remote_copy(
            src_ref=w.full.at[m, core], dst_ref=w.full.at[m, core],
            send_sem=w.swap_ssem.at[m], recv_sem=w.swap_rsem.at[m],
            device_id={"dom": partner}, device_id_type=MESH)

    def cross_copy():
        return pltpu.make_async_remote_copy(
            src_ref=w.cross_send, dst_ref=w.cross_recv,
            send_sem=w.cross_ssem, recv_sem=w.cross_rsem,
            device_id={"band": other}, device_id_type=MESH)

    def put_sums(m, value):
        w.sums[m] = value.reshape(2, W // 2, W)

    def pair_up(m):
        core_copy(m).wait()
        total = w.sums[m, core] + w.core_recv[m]
        w.pair[m] = total.reshape(n, chunk, W)

    def own_total(m):
        wait_all(scatter_copies(m))
        total = w.pair[m, chip]
        for j in range(n - 1):
            total = total + w.scat_recv[m, j]
        return total

    band_copy(0, other).start()
    high, low = halves(band_ref[...])
    def fill(ref, value):
        count, size = value.shape[0], ref.shape[0]
        ref[pl.ds(0, count), :] = value
        if size > count:
            ref[pl.ds(count, size - count), :] = jnp.zeros((size - count, W), bf16)

    fill(w.near_high, high)
    fill(w.near_low, low)
    turned_high, turned_low = halves(jnp.transpose(w.bands[...]))
    put_sums(0, dot(turned_high, w.near_high[...])
             + dot(turned_high, w.near_low[...])
             + dot(turned_low, w.near_high[...]))
    core_copy(0).start()
    pair_up(0)
    start_all(scatter_copies(0))
    same = own_total(0)
    w.full[0, core, chip, pl.ds(0, chunk), :] = same
    squares = (same * same).reshape(chunk // 8, 8, W).sum(0)
    w.full[0, core, chip, pl.ds(chunk, 8), :] = squares
    start_all(gather_copies(0))

    band_copy(0, other).wait_send()
    band_copy(0, band).wait_recv()
    band_copy(1, band).start()
    rows = pl.ds(pl.multiple_of(band * half, 16), half)
    far_high, far_low = halves(w.far_band[rows, :])
    near_high, near_low = w.near_high[rows, :], w.near_low[rows, :]
    first = band == 0

    def pick(a, b):
        return jnp.where(first, a, b)

    fill(w.left_high, pick(far_high, near_high))
    fill(w.left_low, pick(far_low, near_low))
    fill(w.right_high, pick(near_high, far_high))
    fill(w.right_low, pick(near_low, far_low))
    put_sums(1, dot_tn(w.left_high[...], w.right_high[...])
             + dot_tn(w.left_high[...], w.right_low[...])
             + dot_tn(w.left_low[...], w.right_high[...]))
    core_copy(1).start()
    pair_up(1)
    start_all(scatter_copies(1))

    wait_all(gather_copies(0))
    swap_copy(0).start()
    cross = own_total(1)
    w.cross_send[pl.ds(0, chunk), :] = cross
    w.cross_send[pl.ds(chunk, 8), :] = squares
    cross_copy().start()
    cross_copy().wait()
    cross = pick(cross, w.cross_recv[pl.ds(0, chunk), :]) + pick(w.cross_recv[pl.ds(0, chunk), :], cross)
    w.full[1, core, chip, pl.ds(0, chunk), :] = cross
    w.full[1, core, chip, pl.ds(chunk, 8), :] = (
        2.0 * (cross * cross).reshape(chunk // 8, 8, W).sum(0) + w.cross_recv[pl.ds(chunk, 8), :])
    start_all(gather_copies(1))
    swap_copy(0).wait()
    near_block = w.full[0, :, :, pl.ds(0, chunk), :].reshape(W, W)
    block_high, block_low = halves(near_block)
    w.block_high[0] = block_high
    w.block_low[0] = block_low
    near_high, near_low = w.near_high[pl.ds(0, s.own), :], w.near_low[pl.ds(0, s.own), :]
    near_wide = dot(near_high, w.block_high[0]) + dot(near_high, w.block_low[0])
    w.near_prod[...] = near_wide + dot(near_low, w.block_high[0])
    band_copy(1, band).wait_send()
    band_copy(1, other).wait_recv()
    high, low = halves(w.far_band[...])
    w.far_high[...] = high
    w.far_low[...] = low
    wait_all(gather_copies(1))
    swap_copy(1).start()
    swap_copy(1).wait()
    total = jnp.sum(w.full[:, :, :, pl.ds(chunk, 8), :])
    norm = jnp.sqrt(jnp.full((1, W), total, f32) + 1e-06)
    far_block = w.full[1, :, :, pl.ds(0, chunk), :].reshape(W, W)
    far_block = pick(far_block, jnp.transpose(far_block))
    block_high, block_low = halves(far_block)
    w.block_high[1] = block_high
    w.block_low[1] = block_low
    wide = dot(w.far_high[...], w.block_high[1]) + dot(w.far_high[...], w.block_low[1])
    wide = wide + dot(w.far_low[...], w.block_high[1]) + w.near_prod[...]
    out_ref[...] = 1.5 * band_ref[...] - wide * (0.5 / norm)


def kernel(s, names, wave_ref, ops_ref, map_ref, face_ref, out_ref, *scratch):
    w = types.SimpleNamespace(**dict(zip(names, scratch)))
    me = lax.axis_index("dom")
    barrier = pltpu.get_barrier_semaphore()
    greeted = [{"dom": lax.rem(me + 1, s.n_dom)}, {"dom": lax.rem(me + s.n_dom - 1, s.n_dom)}]
    if s.gram:
        chip, core = me // 2, lax.rem(me, 2)
        greeted.append({"dom": chip * 2 + (1 - core)})
        greeted.append({"band": 1 - lax.axis_index("band")})
        for j in range(1, s.chips):
            greeted.append({"dom": lax.rem(chip + j, s.chips) * 2 + core})
    for device in greeted:
        pl.semaphore_signal(barrier, inc=1, device_id=device, device_id_type=MESH)

    def ready():
        pl.semaphore_wait(barrier, len(greeted))

    if s.gram:
        if s.own_pad > s.own:
            w.bands[pl.ds(s.own, s.own_pad - s.own), :] = jnp.zeros((s.own_pad - s.own, s.width), f32)
        owned = w.bands.at[pl.ds(0, s.own), :]
        filter_steps(s, ready, wave_ref, ops_ref, map_ref, face_ref, owned, w)
        gram_steps(s, owned, out_ref, w)
    else:
        filter_steps(s, ready, wave_ref, ops_ref, map_ref, face_ref, out_ref, w)


def scratch_of(s):
    C, R, L, W, n, chunk = s.cells, s.rows, s.lanes, s.width, s.chips, s.chunk
    V, dma = pltpu.VMEM, pltpu.SemaphoreType.DMA
    scratch = dict(
        index=V((128, max(L, s.face_pad)), f32),
        face_rows=V((s.face, s.own_pad), bf16),
        vec=V((s.own_pad, 2 * W), bf16),
        take_own=V((C, R, s.own_pad), bf16),
        take_face=V((C, R, s.face_pad), bf16),
        put_own=V((s.own, C * L), bf16),
        put_face=V((s.face, C * L), bf16),
        put_back=V((s.own, s.face_pad), bf16),
        op_pad=V((C, R, L), f32),
        op_high=V((C, R, L), bf16),
        op_low=V((C, R, L), bf16),
        part=V((C, R, 2 * W), f32),
        cell=V((C, L, 2 * W), bf16),
        prod=V((C * L, 2 * W), bf16),
        far=V((s.face_pad, 2 * W), bf16),
        latest=V((s.own, W), f32),
        older=V((s.own, W) if DEGREE > 2 else (8, 128), f32),
        face_send=V((DEGREE, s.face, W), f32),
        face_recv=V((DEGREE, s.face, W), f32),
        back_send=V((DEGREE, s.face, W), f32),
        back_recv=V((DEGREE, s.face, W), f32),
        face_ssem=dma((DEGREE,)),
        face_rsem=dma((DEGREE,)),
        back_ssem=dma((DEGREE,)),
        back_rsem=dma((DEGREE,)),
    )
    if s.gram:
        scratch |= dict(
            bands=V((s.own_pad, W), f32),
            far_band=V((s.own, W), f32),
            near_high=V((s.own_pad, W), bf16),
            near_low=V((s.own_pad, W), bf16),
            left_high=V((s.half_pad, W), bf16),
            left_low=V((s.half_pad, W), bf16),
            right_high=V((s.half_pad, W), bf16),
            right_low=V((s.half_pad, W), bf16),
            far_high=V((s.own, W), bf16),
            far_low=V((s.own, W), bf16),
            near_prod=V((s.own, W), f32),
            block_high=V((2, W, W), bf16),
            block_low=V((2, W, W), bf16),
            sums=V((2, 2, W // 2, W), f32),
            core_recv=V((2, W // 2, W), f32),
            pair=V((2, n, chunk, W), f32),
            scat_recv=V((2, n - 1, chunk, W), f32),
            full=V((2, 2, n, s.packet, W), f32),
            cross_send=V((s.packet, W), f32),
            cross_recv=V((s.packet, W), f32),
            cross_ssem=dma,
            cross_rsem=dma,
            band_ssem=dma((2,)),
            band_rsem=dma((2,)),
            core_ssem=dma((2,)),
            core_rsem=dma((2,)),
            swap_ssem=dma((2,)),
            swap_rsem=dma((2,)),
            scat_ssem=dma((2, n - 1)),
            scat_rsem=dma((2, n - 1)),
            gath_ssem=dma((2, n - 1)),
            gath_rsem=dma((2, n - 1)),
        )
    return scratch


def on_device(wavefun, cell_ops, cell_map, face_list):
    s = Sizes(lax.axis_size("dom"), lax.axis_size("band"), wavefun.shape[0], wavefun.shape[1],
              cell_map.shape[0], cell_map.shape[1], face_list.shape[0])
    scratch = scratch_of(s)
    latest = pl.pallas_call(
        functools.partial(kernel, s, list(scratch)),
        out_shape=jax.ShapeDtypeStruct(wavefun.shape, f32),
        in_specs=[pl.BlockSpec(memory_space=pltpu.VMEM)] * 4,
        out_specs=pl.BlockSpec(memory_space=pltpu.VMEM),
        scratch_shapes=list(scratch.values()),
        compiler_params=pltpu.CompilerParams(
            collective_id=0, has_side_effects=True, vmem_limit_bytes=60 * 1024 * 1024),
        name="filtered_bands",
    )(wavefun, cell_ops, cell_map, face_list.reshape(1, -1))
    if s.gram:
        return latest
    full_bands = lax.all_gather(latest, "band", axis=1, tiled=True)
    partial_value = jnp.einsum("nb,nc->bc", full_bands, full_bands, precision=lax.Precision.HIGHEST)
    margin = lax.psum(partial_value, "dom")
    norm_value = jnp.sqrt(jnp.sum(margin * margin) + 1e-06)
    full_width = margin.shape[0]
    offset = lax.axis_index("band") * s.width
    scaled_cols = lax.dynamic_slice_in_dim(margin, offset, s.width, 1) / norm_value
    identity_cols = lax.dynamic_slice_in_dim(
        jnp.eye(full_width, dtype=jnp.float32), offset, s.width, 1
    )
    mixing = (3.0 * identity_cols - scaled_cols) / 2.0
    return jnp.dot(full_bands, mixing, precision=lax.Precision.HIGHEST)


def solution(mesh):
    return jax.shard_map(
        on_device,
        mesh=mesh,
        in_specs=(P("dom", "band"), P("dom", None, None), P("dom", None), P("dom")),
        out_specs=P("dom", "band"),
        check_vma=False,
    )
```

```python
import functools
import types

import jax
import jax.numpy as jnp
from jax import lax
from jax.experimental import pallas as pl
from jax.experimental.pallas import tpu as pltpu
from jax.sharding import PartitionSpec as P

DEGREE = 2


cheb_centre = 1.0
cheb_half = 1.6

f32 = jnp.float32
bf16 = jnp.bfloat16
MESH = pl.DeviceIdType.MESH


def round_up(value, step):
    return (value + step - 1) // step * step


def halves(value):
    high = value.astype(bf16)
    low = (value - high.astype(f32)).astype(bf16)
    return high, low


def dot(left, right):
    return jnp.dot(left, right, preferred_element_type=f32)


def dot_tn(left, right):
    return lax.dot_general(left, right, (((0,), (0,)), ((), ())), preferred_element_type=f32)


def dot_nt(left, right):
    return lax.dot_general(left, right, (((1,), (1,)), ((), ())), preferred_element_type=f32)


class Sizes:
    def __init__(self, n_dom, n_band, own, width, cells, nodes, face):
        self.n_dom, self.n_band = n_dom, n_band
        self.own, self.width = own, width
        self.cells, self.nodes, self.face = cells, nodes, face
        self.own_pad = round_up(own, 128)
        self.face_pad = round_up(face, 128)
        self.rows = round_up(nodes, 16)
        self.lanes = round_up(nodes, 128)
        self.half_pad = round_up(own // 2, 128)
        self.chips = n_dom // 2
        self.chunk = width // n_dom
        self.packet = self.chunk + 8
        self.gram = (
            n_band == 2
            and n_dom % 2 == 0
            and n_dom > 2
            and width % (8 * n_dom) == 0
            and width % 128 == 0
            and own % 32 == 0
        )


def start_all(copies):
    for copy in copies:
        copy.start()


def wait_all(copies):
    for copy in copies:
        copy.wait()


def filter_steps(s, ready, wave_ref, ops_ref, map_ref, face_ref, result_ref, w):
    me = lax.axis_index("dom")
    right = lax.rem(me + 1, s.n_dom)
    left = lax.rem(me + s.n_dom - 1, s.n_dom)
    C, R, L, W = s.cells, s.rows, s.lanes, s.width

    def split_store(ref, first, value):
        high, low = halves(value)
        ref[pl.ds(first, value.shape[0]), pl.ds(0, W)] = high
        ref[pl.ds(first, value.shape[0]), pl.ds(W, W)] = low

    def merged(wide):
        return wide[:, :W] + wide[:, W:]

    def ops_copy(c):
        return pltpu.make_async_copy(ops_ref.at[c], w.ops.at[c], w.ops_sem.at[c])

    for c in range(C):
        ops_copy(c).start()

    w.index[...] = jnp.full(w.index.shape, -1.0, f32)
    w.index[pl.ds(0, C), pl.ds(0, s.nodes)] = map_ref[...].astype(f32)
    w.index[pl.ds(C, 1), pl.ds(0, s.face)] = face_ref[...].astype(f32)
    columns = jnp.transpose(w.index[...])

    def one_hot(match):
        return jnp.where(match, 1.0, 0.0).astype(bf16)

    def iota(shape, axis):
        return lax.broadcasted_iota(jnp.int32, shape, axis).astype(f32)

    w.face_rows[...] = one_hot(columns[: s.face, C : C + 1] == iota((s.face, s.own_pad), 1))
    w.vec[pl.ds(s.own, s.own_pad - s.own), :] = jnp.zeros((s.own_pad - s.own, 2 * W), bf16)
    split_store(w.vec, 0, wave_ref[...])

    def face_copy(step):
        return pltpu.make_async_remote_copy(
            src_ref=w.face_send.at[step], dst_ref=w.face_recv.at[step],
            send_sem=w.face_ssem.at[step], recv_sem=w.face_rsem.at[step],
            device_id={"dom": left}, device_id_type=MESH)

    def back_copy(step):
        return pltpu.make_async_remote_copy(
            src_ref=w.back_send.at[step], dst_ref=w.back_recv.at[step],
            send_sem=w.back_ssem.at[step], recv_sem=w.back_rsem.at[step],
            device_id={"dom": right}, device_id_type=MESH)

    w.face_send[0] = merged(dot(w.face_rows[...], w.vec[...]))
    ready()
    face_copy(0).start()

    w.op_pad[...] = jnp.zeros(w.op_pad.shape, f32)
    for c in range(C):
        column = columns[:R, c : c + 1]
        w.take_own[c] = one_hot(column == iota((R, s.own_pad), 1))
        w.take_face[c] = one_hot(column - float(s.own) == iota((R, s.face_pad), 1))
        row = w.index[c : c + 1, :]
        w.put_own[:, pl.ds(c * L, L)] = one_hot(row == iota((s.own, L), 0))
        w.put_face[:, pl.ds(c * L, L)] = one_hot(row - float(s.own) == iota((s.face, L), 0))
        ops_copy(c).wait()
        w.op_pad[c, pl.ds(0, s.nodes), pl.ds(0, s.nodes)] = w.ops[c]
        high, low = halves(w.op_pad[c])
        w.op_high[c] = high
        w.op_low[c] = low
        if L > R:
            w.prod[pl.ds(c * L + R, L - R), :] = jnp.zeros((L - R, 2 * W), bf16)
            w.cell[c, pl.ds(R, L - R), :] = jnp.zeros((L - R, 2 * W), bf16)
    w.put_back[...] = one_hot(w.index[C : C + 1, pl.ds(0, s.face_pad)] == iota((s.own, s.face_pad), 0))
    if s.face_pad > s.face:
        w.far[pl.ds(s.face, s.face_pad - s.face), :] = jnp.zeros((s.face_pad - s.face, 2 * W), bf16)

    for step in range(DEGREE):
        if step > 0:
            split_store(w.vec, 0, w.latest[...])
            w.face_send[step] = merged(dot(w.face_rows[...], w.vec[...]))
            face_copy(step).start()
        for c in range(C):
            w.part[c] = dot(w.take_own[c], w.vec[...])
        face_copy(step).wait()
        split_store(w.far, 0, w.face_recv[step])
        for c in range(C):
            cell = w.part[c] + dot(w.take_face[c], w.far[...])
            w.cell[c, pl.ds(0, R), :] = cell.astype(bf16)
            wide = dot(w.op_high[c], w.cell[c])
            value = wide[:, :W] + wide[:, W:] + dot(w.op_low[c], w.cell[c, :, pl.ds(0, W)])
            split_store(w.prod, c * L, value)
        w.back_send[step] = merged(dot(w.put_face[...], w.prod[...]))
        back_copy(step).start()
        applied = merged(dot(w.put_own[...], w.prod[...]))
        back_copy(step).wait()
        split_store(w.far, 0, w.back_recv[step])
        applied = applied + merged(dot(w.put_back[...], w.far[...]))
        current = wave_ref[...] if step == 0 else w.latest[...]
        if step == 0:
            following = (applied - cheb_centre * current) / cheb_half
        else:
            earlier = wave_ref[...] if step == 1 else w.older[...]
            following = 2.0 * (applied - cheb_centre * current) / cheb_half - earlier
        if step == DEGREE - 1:
            result_ref[...] = following
        else:
            if step > 0 and step < DEGREE - 1:
                w.older[...] = current
            w.latest[...] = following


def gram_steps(s, band_ref, out_ref, w):
    me = lax.axis_index("dom")
    band = lax.axis_index("band")
    other = 1 - band
    chip, core = me // 2, lax.rem(me, 2)
    partner = chip * 2 + (1 - core)
    W, half, n, chunk = s.width, s.own // 2, s.chips, s.chunk

    def band_copy(turn, first):
        rows = pl.ds(pl.multiple_of(first * half, 8), half)
        return pltpu.make_async_remote_copy(
            src_ref=band_ref.at[rows, :], dst_ref=w.far_band.at[rows, :],
            send_sem=w.band_ssem.at[turn], recv_sem=w.band_rsem.at[turn],
            device_id={"band": other}, device_id_type=MESH)

    def core_copy(m):
        return pltpu.make_async_remote_copy(
            src_ref=w.sums.at[m, 1 - core], dst_ref=w.core_recv.at[m],
            send_sem=w.core_ssem.at[m], recv_sem=w.core_rsem.at[m],
            device_id={"dom": partner}, device_id_type=MESH)

    def scatter_copies(m):
        copies = []
        for j in range(1, n):
            target = lax.rem(chip + j, n)
            copies.append(pltpu.make_async_remote_copy(
                src_ref=w.pair.at[m, target], dst_ref=w.scat_recv.at[m, j - 1],
                send_sem=w.scat_ssem.at[m, j - 1], recv_sem=w.scat_rsem.at[m, j - 1],
                device_id={"dom": target * 2 + core}, device_id_type=MESH))
        return copies

    def gather_copies(m):
        copies = []
        for j in range(1, n):
            target = lax.rem(chip + j, n)
            copies.append(pltpu.make_async_remote_copy(
                src_ref=w.full.at[m, core, chip], dst_ref=w.full.at[m, core, chip],
                send_sem=w.gath_ssem.at[m, j - 1], recv_sem=w.gath_rsem.at[m, j - 1],
                device_id={"dom": target * 2 + core}, device_id_type=MESH))
        return copies

    def swap_copy(m):
        return pltpu.make_async_remote_copy(
            src_ref=w.full.at[m, core], dst_ref=w.full.at[m, core],
            send_sem=w.swap_ssem.at[m], recv_sem=w.swap_rsem.at[m],
            device_id={"dom": partner}, device_id_type=MESH)

    def cross_copy():
        return pltpu.make_async_remote_copy(
            src_ref=w.cross_send, dst_ref=w.cross_recv,
            send_sem=w.cross_ssem, recv_sem=w.cross_rsem,
            device_id={"band": other}, device_id_type=MESH)

    def put_sums(m, value):
        w.sums[m] = value.reshape(2, W // 2, W)

    def pair_up(m):
        core_copy(m).wait()
        total = w.sums[m, core] + w.core_recv[m]
        w.pair[m] = total.reshape(n, chunk, W)

    def own_total(m):
        wait_all(scatter_copies(m))
        total = w.pair[m, chip]
        for j in range(n - 1):
            total = total + w.scat_recv[m, j]
        return total

    band_copy(0, other).start()
    high, low = halves(band_ref[...])
    def fill(ref, value):
        count, size = value.shape[0], ref.shape[0]
        ref[pl.ds(0, count), :] = value
        if size > count:
            ref[pl.ds(count, size - count), :] = jnp.zeros((size - count, W), bf16)

    fill(w.near_high, high)
    fill(w.near_low, low)
    turned_high, turned_low = halves(jnp.transpose(w.bands[...]))
    put_sums(0, dot(turned_high, w.near_high[...])
             + dot(turned_high, w.near_low[...])
             + dot(turned_low, w.near_high[...]))
    core_copy(0).start()
    pair_up(0)
    start_all(scatter_copies(0))
    same = own_total(0)
    w.full[0, core, chip, pl.ds(0, chunk), :] = same
    squares = (same * same).reshape(chunk // 8, 8, W).sum(0)
    w.full[0, core, chip, pl.ds(chunk, 8), :] = squares
    start_all(gather_copies(0))

    band_copy(0, other).wait_send()
    band_copy(0, band).wait_recv()
    band_copy(1, band).start()
    rows = pl.ds(pl.multiple_of(band * half, 16), half)
    far_high, far_low = halves(w.far_band[rows, :])
    near_high, near_low = w.near_high[rows, :], w.near_low[rows, :]
    first = band == 0

    def pick(a, b):
        return jnp.where(first, a, b)

    fill(w.left_high, pick(far_high, near_high))
    fill(w.left_low, pick(far_low, near_low))
    fill(w.right_high, pick(near_high, far_high))
    fill(w.right_low, pick(near_low, far_low))
    put_sums(1, dot_tn(w.left_high[...], w.right_high[...])
             + dot_tn(w.left_high[...], w.right_low[...])
             + dot_tn(w.left_low[...], w.right_high[...]))
    core_copy(1).start()
    pair_up(1)
    start_all(scatter_copies(1))

    wait_all(gather_copies(0))
    swap_copy(0).start()
    cross = own_total(1)
    w.cross_send[pl.ds(0, chunk), :] = cross
    w.cross_send[pl.ds(chunk, 8), :] = squares
    cross_copy().start()
    cross_copy().wait()
    cross = pick(cross, w.cross_recv[pl.ds(0, chunk), :]) + pick(w.cross_recv[pl.ds(0, chunk), :], cross)
    w.full[1, core, chip, pl.ds(0, chunk), :] = cross
    w.full[1, core, chip, pl.ds(chunk, 8), :] = (
        2.0 * (cross * cross).reshape(chunk // 8, 8, W).sum(0) + w.cross_recv[pl.ds(chunk, 8), :])
    start_all(gather_copies(1))
    swap_copy(0).wait()
    near_block = w.full[0, :, :, pl.ds(0, chunk), :].reshape(W, W)
    block_high, block_low = halves(near_block)
    w.block_high[0] = block_high
    w.block_low[0] = block_low
    near_high, near_low = w.near_high[pl.ds(0, s.own), :], w.near_low[pl.ds(0, s.own), :]
    near_wide = dot(near_high, w.block_high[0]) + dot(near_high, w.block_low[0])
    w.near_prod[...] = near_wide + dot(near_low, w.block_high[0])
    band_copy(1, band).wait_send()
    band_copy(1, other).wait_recv()
    high, low = halves(w.far_band[...])
    w.far_high[...] = high
    w.far_low[...] = low
    wait_all(gather_copies(1))
    swap_copy(1).start()
    swap_copy(1).wait()
    total = jnp.sum(w.full[:, :, :, pl.ds(chunk, 8), :])
    norm = jnp.sqrt(jnp.full((1, W), total, f32) + 1e-06)
    far_block = w.full[1, :, :, pl.ds(0, chunk), :].reshape(W, W)
    far_block = pick(far_block, jnp.transpose(far_block))
    block_high, block_low = halves(far_block)
    w.block_high[1] = block_high
    w.block_low[1] = block_low
    wide = dot(w.far_high[...], w.block_high[1]) + dot(w.far_high[...], w.block_low[1])
    wide = wide + dot(w.far_low[...], w.block_high[1]) + w.near_prod[...]
    out_ref[...] = 1.5 * band_ref[...] - wide * (0.5 / norm)


def kernel(s, names, wave_ref, ops_ref, map_ref, face_ref, out_ref, *scratch):
    w = types.SimpleNamespace(**dict(zip(names, scratch)))
    me = lax.axis_index("dom")
    barrier = pltpu.get_barrier_semaphore()
    greeted = [{"dom": lax.rem(me + 1, s.n_dom)}, {"dom": lax.rem(me + s.n_dom - 1, s.n_dom)}]
    if s.gram:
        chip, core = me // 2, lax.rem(me, 2)
        greeted.append({"dom": chip * 2 + (1 - core)})
        greeted.append({"band": 1 - lax.axis_index("band")})
        for j in range(1, s.chips):
            greeted.append({"dom": lax.rem(chip + j, s.chips) * 2 + core})
    for device in greeted:
        pl.semaphore_signal(barrier, inc=1, device_id=device, device_id_type=MESH)

    def ready():
        pl.semaphore_wait(barrier, len(greeted))

    if s.gram:
        if s.own_pad > s.own:
            w.bands[pl.ds(s.own, s.own_pad - s.own), :] = jnp.zeros((s.own_pad - s.own, s.width), f32)
        owned = w.bands.at[pl.ds(0, s.own), :]
        filter_steps(s, ready, wave_ref, ops_ref, map_ref, face_ref, owned, w)
        gram_steps(s, owned, out_ref, w)
    else:
        filter_steps(s, ready, wave_ref, ops_ref, map_ref, face_ref, out_ref, w)


def scratch_of(s):
    C, R, L, W, n, chunk = s.cells, s.rows, s.lanes, s.width, s.chips, s.chunk
    V, dma = pltpu.VMEM, pltpu.SemaphoreType.DMA
    scratch = dict(
        index=V((128, max(L, s.face_pad)), f32),
        face_rows=V((s.face, s.own_pad), bf16),
        vec=V((s.own_pad, 2 * W), bf16),
        take_own=V((C, R, s.own_pad), bf16),
        take_face=V((C, R, s.face_pad), bf16),
        put_own=V((s.own, C * L), bf16),
        put_face=V((s.face, C * L), bf16),
        put_back=V((s.own, s.face_pad), bf16),
        ops=V((C, s.nodes, s.nodes), f32),
        ops_sem=dma((C,)),
        op_pad=V((C, R, L), f32),
        op_high=V((C, R, L), bf16),
        op_low=V((C, R, L), bf16),
        part=V((C, R, 2 * W), f32),
        cell=V((C, L, 2 * W), bf16),
        prod=V((C * L, 2 * W), bf16),
        far=V((s.face_pad, 2 * W), bf16),
        latest=V((s.own, W), f32),
        older=V((s.own, W) if DEGREE > 2 else (8, 128), f32),
        face_send=V((DEGREE, s.face, W), f32),
        face_recv=V((DEGREE, s.face, W), f32),
        back_send=V((DEGREE, s.face, W), f32),
        back_recv=V((DEGREE, s.face, W), f32),
        face_ssem=dma((DEGREE,)),
        face_rsem=dma((DEGREE,)),
        back_ssem=dma((DEGREE,)),
        back_rsem=dma((DEGREE,)),
    )
    if s.gram:
        scratch |= dict(
            bands=V((s.own_pad, W), f32),
            far_band=V((s.own, W), f32),
            near_high=V((s.own_pad, W), bf16),
            near_low=V((s.own_pad, W), bf16),
            left_high=V((s.half_pad, W), bf16),
            left_low=V((s.half_pad, W), bf16),
            right_high=V((s.half_pad, W), bf16),
            right_low=V((s.half_pad, W), bf16),
            far_high=V((s.own, W), bf16),
            far_low=V((s.own, W), bf16),
            near_prod=V((s.own, W), f32),
            block_high=V((2, W, W), bf16),
            block_low=V((2, W, W), bf16),
            sums=V((2, 2, W // 2, W), f32),
            core_recv=V((2, W // 2, W), f32),
            pair=V((2, n, chunk, W), f32),
            scat_recv=V((2, n - 1, chunk, W), f32),
            full=V((2, 2, n, s.packet, W), f32),
            cross_send=V((s.packet, W), f32),
            cross_recv=V((s.packet, W), f32),
            cross_ssem=dma,
            cross_rsem=dma,
            band_ssem=dma((2,)),
            band_rsem=dma((2,)),
            core_ssem=dma((2,)),
            core_rsem=dma((2,)),
            swap_ssem=dma((2,)),
            swap_rsem=dma((2,)),
            scat_ssem=dma((2, n - 1)),
            scat_rsem=dma((2, n - 1)),
            gath_ssem=dma((2, n - 1)),
            gath_rsem=dma((2, n - 1)),
        )
    return scratch


def on_device(wavefun, cell_ops, cell_map, face_list):
    s = Sizes(lax.axis_size("dom"), lax.axis_size("band"), wavefun.shape[0], wavefun.shape[1],
              cell_map.shape[0], cell_map.shape[1], face_list.shape[0])
    scratch = scratch_of(s)
    latest = pl.pallas_call(
        functools.partial(kernel, s, list(scratch)),
        out_shape=jax.ShapeDtypeStruct(wavefun.shape, f32),
        in_specs=[pl.BlockSpec(memory_space=space) for space in (pltpu.VMEM, pl.ANY, pltpu.VMEM, pltpu.VMEM)],
        out_specs=pl.BlockSpec(memory_space=pltpu.VMEM),
        scratch_shapes=list(scratch.values()),
        compiler_params=pltpu.CompilerParams(
            collective_id=0, has_side_effects=True, vmem_limit_bytes=60 * 1024 * 1024),
        name="filtered_bands",
    )(wavefun, cell_ops, cell_map, face_list.reshape(1, -1))
    if s.gram:
        return latest
    full_bands = lax.all_gather(latest, "band", axis=1, tiled=True)
    partial_value = jnp.einsum("nb,nc->bc", full_bands, full_bands, precision=lax.Precision.HIGHEST)
    margin = lax.psum(partial_value, "dom")
    norm_value = jnp.sqrt(jnp.sum(margin * margin) + 1e-06)
    full_width = margin.shape[0]
    offset = lax.axis_index("band") * s.width
    scaled_cols = lax.dynamic_slice_in_dim(margin, offset, s.width, 1) / norm_value
    identity_cols = lax.dynamic_slice_in_dim(
        jnp.eye(full_width, dtype=jnp.float32), offset, s.width, 1
    )
    mixing = (3.0 * identity_cols - scaled_cols) / 2.0
    return jnp.dot(full_bands, mixing, precision=lax.Precision.HIGHEST)


def solution(mesh):
    return jax.shard_map(
        on_device,
        mesh=mesh,
        in_specs=(P("dom", "band"), P("dom", None, None), P("dom", None), P("dom")),
        out_specs=P("dom", "band"),
        check_vma=False,
    )
```

```python
import functools
import types

import jax
import jax.numpy as jnp
from jax import lax
from jax.experimental import pallas as pl
from jax.experimental.pallas import tpu as pltpu
from jax.sharding import PartitionSpec as P

DEGREE = 2


cheb_centre = 1.0
cheb_half = 1.6

f32 = jnp.float32
bf16 = jnp.bfloat16
MESH = pl.DeviceIdType.MESH


def round_up(value, step):
    return (value + step - 1) // step * step


def halves(value):
    high = value.astype(bf16)
    low = (value - high.astype(f32)).astype(bf16)
    return high, low


def dot(left, right):
    return jnp.dot(left, right, preferred_element_type=f32)


def dot_tn(left, right):
    return lax.dot_general(left, right, (((0,), (0,)), ((), ())), preferred_element_type=f32)


def dot_nt(left, right):
    return lax.dot_general(left, right, (((1,), (1,)), ((), ())), preferred_element_type=f32)


class Sizes:
    def __init__(self, n_dom, n_band, own, width, cells, nodes, face):
        self.n_dom, self.n_band = n_dom, n_band
        self.own, self.width = own, width
        self.cells, self.nodes, self.face = cells, nodes, face
        self.own_pad = round_up(own, 128)
        self.face_pad = round_up(face, 128)
        self.rows = round_up(nodes, 16)
        self.lanes = round_up(nodes, 128)
        self.blocks = 2 if width % 256 == 0 else 1
        self.block = width // self.blocks
        self.half_pad = round_up(own // 2, 128)
        self.chips = n_dom // 2
        self.chunk = width // n_dom
        self.packet = self.chunk + 8
        self.gram = (
            n_band == 2
            and n_dom % 2 == 0
            and n_dom > 2
            and width % (8 * n_dom) == 0
            and width % 128 == 0
            and own % 32 == 0
        )


def start_all(copies):
    for copy in copies:
        copy.start()


def wait_all(copies):
    for copy in copies:
        copy.wait()


def filter_steps(s, ready, done, wave_ref, ops_ref, map_ref, face_ref, result_ref, w):
    me = lax.axis_index("dom")
    right = lax.rem(me + 1, s.n_dom)
    left = lax.rem(me + s.n_dom - 1, s.n_dom)
    C, R, L, W = s.cells, s.rows, s.lanes, s.block

    def split_store(ref, first, value):
        high, low = halves(value)
        ref[pl.ds(first, value.shape[0]), pl.ds(0, W)] = high
        ref[pl.ds(first, value.shape[0]), pl.ds(W, W)] = low

    def merged(wide):
        return wide[:, :W] + wide[:, W:]

    def ops_copy(c):
        return pltpu.make_async_copy(ops_ref.at[c], w.ops.at[c], w.ops_sem.at[c])

    for c in range(C):
        ops_copy(c).start()

    w.index[...] = jnp.full(w.index.shape, -1.0, f32)
    w.index[pl.ds(0, C), pl.ds(0, s.nodes)] = map_ref[...].astype(f32)
    w.index[pl.ds(C, 1), pl.ds(0, s.face)] = face_ref[...].astype(f32)
    columns = jnp.transpose(w.index[...])

    def one_hot(match):
        return jnp.where(match, 1.0, 0.0).astype(bf16)

    def iota(shape, axis):
        return lax.broadcasted_iota(jnp.int32, shape, axis).astype(f32)

    w.face_rows[...] = one_hot(columns[: s.face, C : C + 1] == iota((s.face, s.own_pad), 1))
    for q in range(s.blocks):
        if s.own_pad > s.own:
            w.vec[q, pl.ds(s.own, s.own_pad - s.own), :] = jnp.zeros((s.own_pad - s.own, 2 * W), bf16)
        split_store(w.vec.at[q], 0, wave_ref[:, pl.ds(q * W, W)])

    def face_copy(step, q):
        return pltpu.make_async_remote_copy(
            src_ref=w.face_send.at[step, q], dst_ref=w.face_recv.at[step, q],
            send_sem=w.face_ssem.at[step, q], recv_sem=w.face_rsem.at[step, q],
            device_id={"dom": left}, device_id_type=MESH)

    def back_copy(step, q):
        return pltpu.make_async_remote_copy(
            src_ref=w.back_send.at[step, q], dst_ref=w.back_recv.at[step, q],
            send_sem=w.back_ssem.at[step, q], recv_sem=w.back_rsem.at[step, q],
            device_id={"dom": right}, device_id_type=MESH)

    def begin(step, q):
        w.face_send[step, q] = merged(dot(w.face_rows[...], w.vec[q]))
        if step == 0 and q == 0:
            ready()
        face_copy(step, q).start()

    for q in range(s.blocks):
        begin(0, q)

    w.op_pad[...] = jnp.zeros(w.op_pad.shape, f32)
    for c in range(C):
        column = columns[:R, c : c + 1]
        w.take_own[c] = one_hot(column == iota((R, s.own_pad), 1))
        w.take_face[c] = one_hot(column - float(s.own) == iota((R, s.face_pad), 1))
        row = w.index[c : c + 1, :]
        w.put_own[:, pl.ds(c * L, L)] = one_hot(row == iota((s.own, L), 0))
        w.put_face[:, pl.ds(c * L, L)] = one_hot(row - float(s.own) == iota((s.face, L), 0))
        ops_copy(c).wait()
        w.op_pad[c, pl.ds(0, s.nodes), pl.ds(0, s.nodes)] = w.ops[c]
        high, low = halves(w.op_pad[c])
        w.op_high[c] = high
        w.op_low[c] = low
        if L > R:
            w.prod[pl.ds(c * L + R, L - R), :] = jnp.zeros((L - R, 2 * W), bf16)
            w.cell[c, pl.ds(R, L - R), :] = jnp.zeros((L - R, 2 * W), bf16)
    w.put_back[...] = one_hot(w.index[C : C + 1, pl.ds(0, s.face_pad)] == iota((s.own, s.face_pad), 0))
    if s.face_pad > s.face:
        for q in range(s.blocks):
            w.far[q, pl.ds(s.face, s.face_pad - s.face), :] = jnp.zeros((s.face_pad - s.face, 2 * W), bf16)

    def gather(step, q):
        for c in range(C):
            w.part[q, c] = dot(w.take_own[c], w.vec[q])

    def middle(step, q):
        face_copy(step, q).wait()
        split_store(w.far.at[q], 0, w.face_recv[step, q])
        for c in range(C):
            cell = w.part[q, c] + dot(w.take_face[c], w.far[q])
            w.cell[c, pl.ds(0, R), :] = cell.astype(bf16)
            wide = dot(w.op_high[c], w.cell[c])
            value = wide[:, :W] + wide[:, W:] + dot(w.op_low[c], w.cell[c, :, pl.ds(0, W)])
            split_store(w.prod, c * L, value)
        w.back_send[step, q] = merged(dot(w.put_face[...], w.prod[...]))
        back_copy(step, q).start()
        w.applied[q] = merged(dot(w.put_own[...], w.prod[...]))

    def finish(step, q):
        back_copy(step, q).wait()
        split_store(w.far.at[q], 0, w.back_recv[step, q])
        applied = w.applied[q] + merged(dot(w.put_back[...], w.far[q]))
        columns = pl.ds(q * W, W)
        if step == 0:
            current = wave_ref[:, columns]
            following = (applied - cheb_centre * current) / cheb_half
        else:
            current = w.latest[:, columns]
            earlier = wave_ref[:, columns] if step == 1 else w.older[:, columns]
            following = 2.0 * (applied - cheb_centre * current) / cheb_half - earlier
        if step == DEGREE - 1:
            result_ref[:, columns] = following
            done(q)
        else:
            if step > 0:
                w.older[:, columns] = current
            w.latest[:, columns] = following
            split_store(w.vec.at[q], 0, following)
            begin(step + 1, q)

    gather(0, 0)
    for step in range(DEGREE):
        last = step == DEGREE - 1
        middle(step, 0)
        if s.blocks > 1:
            gather(step, 1)
        finish(step, 0)
        if s.blocks > 1:
            middle(step, 1)
        if not last:
            gather(step + 1, 0)
        if s.blocks > 1:
            finish(step, 1)


def band_copy(s, band_ref, w, turn, first, q):
    half = s.own // 2
    rows = pl.ds(pl.multiple_of(first * half, 8), half)
    columns = pl.ds(q * s.block, s.block)
    return pltpu.make_async_remote_copy(
        src_ref=band_ref.at[rows, columns], dst_ref=w.far_band.at[rows, columns],
        send_sem=w.band_ssem.at[turn, q], recv_sem=w.band_rsem.at[turn, q],
        device_id={"band": 1 - lax.axis_index("band")}, device_id_type=MESH)


def gram_steps(s, band_ref, out_ref, w):
    me = lax.axis_index("dom")
    band = lax.axis_index("band")
    other = 1 - band
    chip, core = me // 2, lax.rem(me, 2)
    partner = chip * 2 + (1 - core)
    W, half, n, chunk = s.width, s.own // 2, s.chips, s.chunk

    def core_copy(m):
        return pltpu.make_async_remote_copy(
            src_ref=w.sums.at[m, 1 - core], dst_ref=w.core_recv.at[m],
            send_sem=w.core_ssem.at[m], recv_sem=w.core_rsem.at[m],
            device_id={"dom": partner}, device_id_type=MESH)

    def scatter_copies(m):
        copies = []
        for j in range(1, n):
            target = lax.rem(chip + j, n)
            copies.append(pltpu.make_async_remote_copy(
                src_ref=w.pair.at[m, target], dst_ref=w.scat_recv.at[m, j - 1],
                send_sem=w.scat_ssem.at[m, j - 1], recv_sem=w.scat_rsem.at[m, j - 1],
                device_id={"dom": target * 2 + core}, device_id_type=MESH))
        return copies

    def gather_copies(m):
        copies = []
        for j in range(1, n):
            target = lax.rem(chip + j, n)
            copies.append(pltpu.make_async_remote_copy(
                src_ref=w.full.at[m, core, chip], dst_ref=w.full.at[m, core, chip],
                send_sem=w.gath_ssem.at[m, j - 1], recv_sem=w.gath_rsem.at[m, j - 1],
                device_id={"dom": target * 2 + core}, device_id_type=MESH))
        return copies

    def swap_copy(m):
        return pltpu.make_async_remote_copy(
            src_ref=w.full.at[m, core], dst_ref=w.full.at[m, core],
            send_sem=w.swap_ssem.at[m], recv_sem=w.swap_rsem.at[m],
            device_id={"dom": partner}, device_id_type=MESH)

    def cross_copy():
        return pltpu.make_async_remote_copy(
            src_ref=w.cross_send, dst_ref=w.cross_recv,
            send_sem=w.cross_ssem, recv_sem=w.cross_rsem,
            device_id={"band": other}, device_id_type=MESH)

    def put_sums(m, value):
        w.sums[m] = value.reshape(2, W // 2, W)

    def pair_up(m):
        core_copy(m).wait()
        total = w.sums[m, core] + w.core_recv[m]
        w.pair[m] = total.reshape(n, chunk, W)

    def own_total(m):
        wait_all(scatter_copies(m))
        total = w.pair[m, chip]
        for j in range(n - 1):
            total = total + w.scat_recv[m, j]
        return total

    high, low = halves(band_ref[...])
    def fill(ref, value):
        count, size = value.shape[0], ref.shape[0]
        ref[pl.ds(0, count), :] = value
        if size > count:
            ref[pl.ds(count, size - count), :] = jnp.zeros((size - count, W), bf16)

    fill(w.near_high, high)
    fill(w.near_low, low)
    turned_high, turned_low = halves(jnp.transpose(w.bands[...]))
    put_sums(0, dot(turned_high, w.near_high[...])
             + dot(turned_high, w.near_low[...])
             + dot(turned_low, w.near_high[...]))
    core_copy(0).start()
    pair_up(0)
    start_all(scatter_copies(0))
    same = own_total(0)
    w.full[0, core, chip, pl.ds(0, chunk), :] = same
    squares = (same * same).reshape(chunk // 8, 8, W).sum(0)
    w.full[0, core, chip, pl.ds(chunk, 8), :] = squares
    start_all(gather_copies(0))

    for q in range(s.blocks):
        band_copy(s, band_ref, w, 0, other, q).wait_send()
        band_copy(s, band_ref, w, 0, band, q).wait_recv()
    for q in range(s.blocks):
        band_copy(s, band_ref, w, 1, band, q).start()
    rows = pl.ds(pl.multiple_of(band * half, 16), half)
    far_high, far_low = halves(w.far_band[rows, :])
    near_high, near_low = w.near_high[rows, :], w.near_low[rows, :]
    first = band == 0

    def pick(a, b):
        return jnp.where(first, a, b)

    fill(w.left_high, pick(far_high, near_high))
    fill(w.left_low, pick(far_low, near_low))
    fill(w.right_high, pick(near_high, far_high))
    fill(w.right_low, pick(near_low, far_low))
    put_sums(1, dot_tn(w.left_high[...], w.right_high[...])
             + dot_tn(w.left_high[...], w.right_low[...])
             + dot_tn(w.left_low[...], w.right_high[...]))
    core_copy(1).start()
    pair_up(1)
    start_all(scatter_copies(1))

    wait_all(gather_copies(0))
    swap_copy(0).start()
    cross = own_total(1)
    w.cross_send[pl.ds(0, chunk), :] = cross
    w.cross_send[pl.ds(chunk, 8), :] = squares
    cross_copy().start()
    cross_copy().wait()
    cross = pick(cross, w.cross_recv[pl.ds(0, chunk), :]) + pick(w.cross_recv[pl.ds(0, chunk), :], cross)
    w.full[1, core, chip, pl.ds(0, chunk), :] = cross
    w.full[1, core, chip, pl.ds(chunk, 8), :] = (
        2.0 * (cross * cross).reshape(chunk // 8, 8, W).sum(0) + w.cross_recv[pl.ds(chunk, 8), :])
    start_all(gather_copies(1))
    swap_copy(0).wait()
    near_block = w.full[0, :, :, pl.ds(0, chunk), :].reshape(W, W)
    block_high, block_low = halves(near_block)
    w.block_high[0] = block_high
    w.block_low[0] = block_low
    near_high, near_low = w.near_high[pl.ds(0, s.own), :], w.near_low[pl.ds(0, s.own), :]
    near_wide = dot(near_high, w.block_high[0]) + dot(near_high, w.block_low[0])
    w.near_prod[...] = near_wide + dot(near_low, w.block_high[0])
    for q in range(s.blocks):
        band_copy(s, band_ref, w, 1, band, q).wait_send()
        band_copy(s, band_ref, w, 1, other, q).wait_recv()
    high, low = halves(w.far_band[...])
    w.far_high[...] = high
    w.far_low[...] = low
    wait_all(gather_copies(1))
    swap_copy(1).start()
    swap_copy(1).wait()
    total = jnp.sum(w.full[:, :, :, pl.ds(chunk, 8), :])
    norm = jnp.sqrt(jnp.full((1, W), total, f32) + 1e-06)
    far_block = w.full[1, :, :, pl.ds(0, chunk), :].reshape(W, W)
    far_block = pick(far_block, jnp.transpose(far_block))
    block_high, block_low = halves(far_block)
    w.block_high[1] = block_high
    w.block_low[1] = block_low
    wide = dot(w.far_high[...], w.block_high[1]) + dot(w.far_high[...], w.block_low[1])
    wide = wide + dot(w.far_low[...], w.block_high[1]) + w.near_prod[...]
    out_ref[...] = 1.5 * band_ref[...] - wide * (0.5 / norm)


def kernel(s, names, wave_ref, ops_ref, map_ref, face_ref, out_ref, *scratch):
    w = types.SimpleNamespace(**dict(zip(names, scratch)))
    me = lax.axis_index("dom")
    barrier = pltpu.get_barrier_semaphore()
    greeted = [{"dom": lax.rem(me + 1, s.n_dom)}, {"dom": lax.rem(me + s.n_dom - 1, s.n_dom)}]
    if s.gram:
        chip, core = me // 2, lax.rem(me, 2)
        greeted.append({"dom": chip * 2 + (1 - core)})
        greeted.append({"band": 1 - lax.axis_index("band")})
        for j in range(1, s.chips):
            greeted.append({"dom": lax.rem(chip + j, s.chips) * 2 + core})
    for device in greeted:
        pl.semaphore_signal(barrier, inc=1, device_id=device, device_id_type=MESH)

    def ready():
        pl.semaphore_wait(barrier, len(greeted))

    if s.gram:
        if s.own_pad > s.own:
            w.bands[pl.ds(s.own, s.own_pad - s.own), :] = jnp.zeros((s.own_pad - s.own, s.width), f32)
        owned = w.bands.at[pl.ds(0, s.own), :]

        def send(q):
            band_copy(s, owned, w, 0, 1 - lax.axis_index("band"), q).start()

        filter_steps(s, ready, send, wave_ref, ops_ref, map_ref, face_ref, owned, w)
        gram_steps(s, owned, out_ref, w)
    else:
        filter_steps(s, ready, lambda q: None, wave_ref, ops_ref, map_ref, face_ref, out_ref, w)


def scratch_of(s):
    C, R, L, W, n, chunk = s.cells, s.rows, s.lanes, s.width, s.chips, s.chunk
    V, dma = pltpu.VMEM, pltpu.SemaphoreType.DMA
    scratch = dict(
        index=V((128, max(L, s.face_pad)), f32),
        face_rows=V((s.face, s.own_pad), bf16),
        vec=V((s.blocks, s.own_pad, 2 * s.block), bf16),
        take_own=V((C, R, s.own_pad), bf16),
        take_face=V((C, R, s.face_pad), bf16),
        put_own=V((s.own, C * L), bf16),
        put_face=V((s.face, C * L), bf16),
        put_back=V((s.own, s.face_pad), bf16),
        ops=V((C, s.nodes, s.nodes), f32),
        ops_sem=dma((C,)),
        op_pad=V((C, R, L), f32),
        op_high=V((C, R, L), bf16),
        op_low=V((C, R, L), bf16),
        part=V((s.blocks, C, R, 2 * s.block), f32),
        applied=V((s.blocks, s.own, s.block), f32),
        cell=V((C, L, 2 * s.block), bf16),
        prod=V((C * L, 2 * s.block), bf16),
        far=V((s.blocks, s.face_pad, 2 * s.block), bf16),
        latest=V((s.own, W), f32),
        older=V((s.own, W) if DEGREE > 2 else (8, 128), f32),
        face_send=V((DEGREE, s.blocks, s.face, s.block), f32),
        face_recv=V((DEGREE, s.blocks, s.face, s.block), f32),
        back_send=V((DEGREE, s.blocks, s.face, s.block), f32),
        back_recv=V((DEGREE, s.blocks, s.face, s.block), f32),
        face_ssem=dma((DEGREE, s.blocks)),
        face_rsem=dma((DEGREE, s.blocks)),
        back_ssem=dma((DEGREE, s.blocks)),
        back_rsem=dma((DEGREE, s.blocks)),
    )
    if s.gram:
        scratch |= dict(
            bands=V((s.own_pad, W), f32),
            far_band=V((s.own, W), f32),
            near_high=V((s.own_pad, W), bf16),
            near_low=V((s.own_pad, W), bf16),
            left_high=V((s.half_pad, W), bf16),
            left_low=V((s.half_pad, W), bf16),
            right_high=V((s.half_pad, W), bf16),
            right_low=V((s.half_pad, W), bf16),
            far_high=V((s.own, W), bf16),
            far_low=V((s.own, W), bf16),
            near_prod=V((s.own, W), f32),
            block_high=V((2, W, W), bf16),
            block_low=V((2, W, W), bf16),
            sums=V((2, 2, W // 2, W), f32),
            core_recv=V((2, W // 2, W), f32),
            pair=V((2, n, chunk, W), f32),
            scat_recv=V((2, n - 1, chunk, W), f32),
            full=V((2, 2, n, s.packet, W), f32),
            cross_send=V((s.packet, W), f32),
            cross_recv=V((s.packet, W), f32),
            cross_ssem=dma,
            cross_rsem=dma,
            band_ssem=dma((2, s.blocks)),
            band_rsem=dma((2, s.blocks)),
            core_ssem=dma((2,)),
            core_rsem=dma((2,)),
            swap_ssem=dma((2,)),
            swap_rsem=dma((2,)),
            scat_ssem=dma((2, n - 1)),
            scat_rsem=dma((2, n - 1)),
            gath_ssem=dma((2, n - 1)),
            gath_rsem=dma((2, n - 1)),
        )
    return scratch


def on_device(wavefun, cell_ops, cell_map, face_list):
    s = Sizes(lax.axis_size("dom"), lax.axis_size("band"), wavefun.shape[0], wavefun.shape[1],
              cell_map.shape[0], cell_map.shape[1], face_list.shape[0])
    scratch = scratch_of(s)
    latest = pl.pallas_call(
        functools.partial(kernel, s, list(scratch)),
        out_shape=jax.ShapeDtypeStruct(wavefun.shape, f32),
        in_specs=[pl.BlockSpec(memory_space=space) for space in (pltpu.VMEM, pl.ANY, pltpu.VMEM, pltpu.VMEM)],
        out_specs=pl.BlockSpec(memory_space=pltpu.VMEM),
        scratch_shapes=list(scratch.values()),
        compiler_params=pltpu.CompilerParams(
            collective_id=0, has_side_effects=True, vmem_limit_bytes=60 * 1024 * 1024),
        name="filtered_bands",
    )(wavefun, cell_ops, cell_map, face_list.reshape(1, -1))
    if s.gram:
        return latest
    full_bands = lax.all_gather(latest, "band", axis=1, tiled=True)
    partial_value = jnp.einsum("nb,nc->bc", full_bands, full_bands, precision=lax.Precision.HIGHEST)
    margin = lax.psum(partial_value, "dom")
    norm_value = jnp.sqrt(jnp.sum(margin * margin) + 1e-06)
    full_width = margin.shape[0]
    offset = lax.axis_index("band") * s.width
    scaled_cols = lax.dynamic_slice_in_dim(margin, offset, s.width, 1) / norm_value
    identity_cols = lax.dynamic_slice_in_dim(
        jnp.eye(full_width, dtype=jnp.float32), offset, s.width, 1
    )
    mixing = (3.0 * identity_cols - scaled_cols) / 2.0
    return jnp.dot(full_bands, mixing, precision=lax.Precision.HIGHEST)


def solution(mesh):
    return jax.shard_map(
        on_device,
        mesh=mesh,
        in_specs=(P("dom", "band"), P("dom", None, None), P("dom", None), P("dom")),
        out_specs=P("dom", "band"),
        check_vma=False,
    )
```

```python
import functools
import types

import jax
import jax.numpy as jnp
from jax import lax
from jax.experimental import pallas as pl
from jax.experimental.pallas import tpu as pltpu
from jax.sharding import PartitionSpec as P

DEGREE = 2


cheb_centre = 1.0
cheb_half = 1.6

f32 = jnp.float32
bf16 = jnp.bfloat16
MESH = pl.DeviceIdType.MESH


def round_up(value, step):
    return (value + step - 1) // step * step


def halves(value):
    high = value.astype(bf16)
    low = (value - high.astype(f32)).astype(bf16)
    return high, low


def dot(left, right):
    return jnp.dot(left, right, preferred_element_type=f32)


def dot_tn(left, right):
    return lax.dot_general(left, right, (((0,), (0,)), ((), ())), preferred_element_type=f32)


def dot_nt(left, right):
    return lax.dot_general(left, right, (((1,), (1,)), ((), ())), preferred_element_type=f32)


class Sizes:
    def __init__(self, n_dom, n_band, own, width, cells, nodes, face):
        self.n_dom, self.n_band = n_dom, n_band
        self.own, self.width = own, width
        self.cells, self.nodes, self.face = cells, nodes, face
        self.own_pad = round_up(own, 128)
        self.face_pad = round_up(face, 128)
        self.rows = round_up(nodes, 16)
        self.lanes = round_up(nodes, 128)
        self.blocks = 2 if width % 256 == 0 else 1
        self.block = width // self.blocks
        self.half_pad = round_up(own // 2, 128)
        self.chips = n_dom // 2
        self.chunk = width // n_dom
        self.packet = self.chunk + 8
        self.gram = (
            n_band == 2
            and n_dom % 2 == 0
            and n_dom > 2
            and width % (8 * n_dom) == 0
            and width % 128 == 0
            and own % 32 == 0
        )


def start_all(copies):
    for copy in copies:
        copy.start()


def wait_all(copies):
    for copy in copies:
        copy.wait()


def filter_steps(s, ready, done, wave_ref, ops_ref, map_ref, face_ref, result_ref, w):
    me = lax.axis_index("dom")
    right = lax.rem(me + 1, s.n_dom)
    left = lax.rem(me + s.n_dom - 1, s.n_dom)
    C, R, L, W = s.cells, s.rows, s.lanes, s.block

    def split_store(ref, first, value):
        high, low = halves(value)
        ref[pl.ds(first, value.shape[0]), pl.ds(0, W)] = high
        ref[pl.ds(first, value.shape[0]), pl.ds(W, W)] = low

    def merged(wide):
        return wide[:, :W] + wide[:, W:]

    ops_copy = pltpu.make_async_copy(ops_ref, w.ops, w.ops_sem)
    ops_copy.start()

    w.index[...] = jnp.full(w.index.shape, -1.0, f32)
    w.index[pl.ds(0, C), pl.ds(0, s.nodes)] = map_ref[...].astype(f32)
    w.index[pl.ds(C, 1), pl.ds(0, s.face)] = face_ref[...].astype(f32)
    columns = jnp.transpose(w.index[...])

    def one_hot(match):
        return jnp.where(match, 1.0, 0.0).astype(bf16)

    def iota(shape, axis):
        return lax.broadcasted_iota(jnp.int32, shape, axis).astype(f32)

    w.face_rows[...] = one_hot(columns[: s.face, C : C + 1] == iota((s.face, s.own_pad), 1))
    for q in range(s.blocks):
        if s.own_pad > s.own:
            w.vec[q, pl.ds(s.own, s.own_pad - s.own), :] = jnp.zeros((s.own_pad - s.own, 2 * W), bf16)
        split_store(w.vec.at[q], 0, wave_ref[:, pl.ds(q * W, W)])

    def face_copy(step, q):
        return pltpu.make_async_remote_copy(
            src_ref=w.face_send.at[step, q], dst_ref=w.face_recv.at[step, q],
            send_sem=w.face_ssem.at[step, q], recv_sem=w.face_rsem.at[step, q],
            device_id={"dom": left}, device_id_type=MESH)

    def back_copy(step, q):
        return pltpu.make_async_remote_copy(
            src_ref=w.back_send.at[step, q], dst_ref=w.back_recv.at[step, q],
            send_sem=w.back_ssem.at[step, q], recv_sem=w.back_rsem.at[step, q],
            device_id={"dom": right}, device_id_type=MESH)

    def begin(step, q):
        w.face_send[step, q] = merged(dot(w.face_rows[...], w.vec[q]))
        if step == 0 and q == 0:
            ready()
        face_copy(step, q).start()

    for q in range(s.blocks):
        begin(0, q)

    w.op_pad[...] = jnp.zeros(w.op_pad.shape, f32)
    for c in range(C):
        column = columns[:R, c : c + 1]
        w.take_own[c] = one_hot(column == iota((R, s.own_pad), 1))
        w.take_face[c] = one_hot(column - float(s.own) == iota((R, s.face_pad), 1))
        row = w.index[c : c + 1, :]
        w.put_own[:, pl.ds(c * L, L)] = one_hot(row == iota((s.own, L), 0))
        w.put_face[:, pl.ds(c * L, L)] = one_hot(row - float(s.own) == iota((s.face, L), 0))
        if c == 0:
            ops_copy.wait()
        w.op_pad[c, pl.ds(0, s.nodes), pl.ds(0, s.nodes)] = w.ops[:, c, :]
        high, low = halves(w.op_pad[c])
        w.op_high[c] = high
        w.op_low[c] = low
        if L > R:
            w.prod[pl.ds(c * L + R, L - R), :] = jnp.zeros((L - R, 2 * W), bf16)
            w.cell[c, pl.ds(R, L - R), :] = jnp.zeros((L - R, 2 * W), bf16)
    w.put_back[...] = one_hot(w.index[C : C + 1, pl.ds(0, s.face_pad)] == iota((s.own, s.face_pad), 0))
    if s.face_pad > s.face:
        for q in range(s.blocks):
            w.far[q, pl.ds(s.face, s.face_pad - s.face), :] = jnp.zeros((s.face_pad - s.face, 2 * W), bf16)

    def gather(step, q):
        for c in range(C):
            w.part[q, c] = dot(w.take_own[c], w.vec[q])

    def middle(step, q):
        face_copy(step, q).wait()
        split_store(w.far.at[q], 0, w.face_recv[step, q])
        for c in range(C):
            cell = w.part[q, c] + dot(w.take_face[c], w.far[q])
            w.cell[c, pl.ds(0, R), :] = cell.astype(bf16)
            wide = dot(w.op_high[c], w.cell[c])
            value = wide[:, :W] + wide[:, W:] + dot(w.op_low[c], w.cell[c, :, pl.ds(0, W)])
            split_store(w.prod, c * L, value)
        w.back_send[step, q] = merged(dot(w.put_face[...], w.prod[...]))
        back_copy(step, q).start()
        w.applied[q] = merged(dot(w.put_own[...], w.prod[...]))

    def finish(step, q):
        back_copy(step, q).wait()
        split_store(w.far.at[q], 0, w.back_recv[step, q])
        applied = w.applied[q] + merged(dot(w.put_back[...], w.far[q]))
        columns = pl.ds(q * W, W)
        if step == 0:
            current = wave_ref[:, columns]
            following = (applied - cheb_centre * current) / cheb_half
        else:
            current = w.latest[:, columns]
            earlier = wave_ref[:, columns] if step == 1 else w.older[:, columns]
            following = 2.0 * (applied - cheb_centre * current) / cheb_half - earlier
        if step == DEGREE - 1:
            result_ref[:, columns] = following
            done(q)
        else:
            if step > 0:
                w.older[:, columns] = current
            w.latest[:, columns] = following
            split_store(w.vec.at[q], 0, following)
            begin(step + 1, q)

    gather(0, 0)
    for step in range(DEGREE):
        last = step == DEGREE - 1
        middle(step, 0)
        if s.blocks > 1:
            gather(step, 1)
        finish(step, 0)
        if s.blocks > 1:
            middle(step, 1)
        if not last:
            gather(step + 1, 0)
        if s.blocks > 1:
            finish(step, 1)


def band_copy(s, band_ref, w, turn, first, q):
    half = s.own // 2
    rows = pl.ds(pl.multiple_of(first * half, 8), half)
    columns = pl.ds(q * s.block, s.block)
    return pltpu.make_async_remote_copy(
        src_ref=band_ref.at[rows, columns], dst_ref=w.far_band.at[rows, columns],
        send_sem=w.band_ssem.at[turn, q], recv_sem=w.band_rsem.at[turn, q],
        device_id={"band": 1 - lax.axis_index("band")}, device_id_type=MESH)


def gram_steps(s, band_ref, out_ref, w):
    me = lax.axis_index("dom")
    band = lax.axis_index("band")
    other = 1 - band
    chip, core = me // 2, lax.rem(me, 2)
    partner = chip * 2 + (1 - core)
    W, half, n, chunk = s.width, s.own // 2, s.chips, s.chunk

    def core_copy(m):
        return pltpu.make_async_remote_copy(
            src_ref=w.sums.at[m, 1 - core], dst_ref=w.core_recv.at[m],
            send_sem=w.core_ssem.at[m], recv_sem=w.core_rsem.at[m],
            device_id={"dom": partner}, device_id_type=MESH)

    def scatter_copies(m):
        copies = []
        for j in range(1, n):
            target = lax.rem(chip + j, n)
            copies.append(pltpu.make_async_remote_copy(
                src_ref=w.pair.at[m, target], dst_ref=w.scat_recv.at[m, j - 1],
                send_sem=w.scat_ssem.at[m, j - 1], recv_sem=w.scat_rsem.at[m, j - 1],
                device_id={"dom": target * 2 + core}, device_id_type=MESH))
        return copies

    def gather_copies(m):
        copies = []
        for j in range(1, n):
            target = lax.rem(chip + j, n)
            copies.append(pltpu.make_async_remote_copy(
                src_ref=w.full.at[m, core, chip], dst_ref=w.full.at[m, core, chip],
                send_sem=w.gath_ssem.at[m, j - 1], recv_sem=w.gath_rsem.at[m, j - 1],
                device_id={"dom": target * 2 + core}, device_id_type=MESH))
        return copies

    def swap_copy(m):
        return pltpu.make_async_remote_copy(
            src_ref=w.full.at[m, core], dst_ref=w.full.at[m, core],
            send_sem=w.swap_ssem.at[m], recv_sem=w.swap_rsem.at[m],
            device_id={"dom": partner}, device_id_type=MESH)

    def cross_copy():
        return pltpu.make_async_remote_copy(
            src_ref=w.cross_send, dst_ref=w.cross_recv,
            send_sem=w.cross_ssem, recv_sem=w.cross_rsem,
            device_id={"band": other}, device_id_type=MESH)

    def put_sums(m, value):
        w.sums[m] = value.reshape(2, W // 2, W)

    def pair_up(m):
        core_copy(m).wait()
        total = w.sums[m, core] + w.core_recv[m]
        w.pair[m] = total.reshape(n, chunk, W)

    def own_total(m):
        wait_all(scatter_copies(m))
        total = w.pair[m, chip]
        for j in range(n - 1):
            total = total + w.scat_recv[m, j]
        return total

    high, low = halves(band_ref[...])
    def fill(ref, value):
        count, size = value.shape[0], ref.shape[0]
        ref[pl.ds(0, count), :] = value
        if size > count:
            ref[pl.ds(count, size - count), :] = jnp.zeros((size - count, W), bf16)

    fill(w.near_high, high)
    fill(w.near_low, low)
    turned_high, turned_low = halves(jnp.transpose(w.bands[...]))
    put_sums(0, dot(turned_high, w.near_high[...])
             + dot(turned_high, w.near_low[...])
             + dot(turned_low, w.near_high[...]))
    core_copy(0).start()
    pair_up(0)
    start_all(scatter_copies(0))
    same = own_total(0)
    w.full[0, core, chip, pl.ds(0, chunk), :] = same
    squares = (same * same).reshape(chunk // 8, 8, W).sum(0)
    w.full[0, core, chip, pl.ds(chunk, 8), :] = squares
    start_all(gather_copies(0))

    for q in range(s.blocks):
        band_copy(s, band_ref, w, 0, other, q).wait_send()
        band_copy(s, band_ref, w, 0, band, q).wait_recv()
    for q in range(s.blocks):
        band_copy(s, band_ref, w, 1, band, q).start()
    rows = pl.ds(pl.multiple_of(band * half, 16), half)
    far_high, far_low = halves(w.far_band[rows, :])
    near_high, near_low = w.near_high[rows, :], w.near_low[rows, :]
    first = band == 0

    def pick(a, b):
        return jnp.where(first, a, b)

    fill(w.left_high, pick(far_high, near_high))
    fill(w.left_low, pick(far_low, near_low))
    fill(w.right_high, pick(near_high, far_high))
    fill(w.right_low, pick(near_low, far_low))
    put_sums(1, dot_tn(w.left_high[...], w.right_high[...])
             + dot_tn(w.left_high[...], w.right_low[...])
             + dot_tn(w.left_low[...], w.right_high[...]))
    core_copy(1).start()
    pair_up(1)
    start_all(scatter_copies(1))

    wait_all(gather_copies(0))
    swap_copy(0).start()
    cross = own_total(1)
    w.cross_send[pl.ds(0, chunk), :] = cross
    w.cross_send[pl.ds(chunk, 8), :] = squares
    cross_copy().start()
    cross_copy().wait()
    cross = pick(cross, w.cross_recv[pl.ds(0, chunk), :]) + pick(w.cross_recv[pl.ds(0, chunk), :], cross)
    w.full[1, core, chip, pl.ds(0, chunk), :] = cross
    w.full[1, core, chip, pl.ds(chunk, 8), :] = (
        2.0 * (cross * cross).reshape(chunk // 8, 8, W).sum(0) + w.cross_recv[pl.ds(chunk, 8), :])
    start_all(gather_copies(1))
    swap_copy(0).wait()
    near_block = w.full[0, :, :, pl.ds(0, chunk), :].reshape(W, W)
    block_high, block_low = halves(near_block)
    w.block_high[0] = block_high
    w.block_low[0] = block_low
    near_high, near_low = w.near_high[pl.ds(0, s.own), :], w.near_low[pl.ds(0, s.own), :]
    near_wide = dot(near_high, w.block_high[0]) + dot(near_high, w.block_low[0])
    w.near_prod[...] = near_wide + dot(near_low, w.block_high[0])
    for q in range(s.blocks):
        band_copy(s, band_ref, w, 1, band, q).wait_send()
        band_copy(s, band_ref, w, 1, other, q).wait_recv()
    high, low = halves(w.far_band[...])
    w.far_high[...] = high
    w.far_low[...] = low
    wait_all(gather_copies(1))
    swap_copy(1).start()
    swap_copy(1).wait()
    total = jnp.sum(w.full[:, :, :, pl.ds(chunk, 8), :])
    norm = jnp.sqrt(jnp.full((1, W), total, f32) + 1e-06)
    far_block = w.full[1, :, :, pl.ds(0, chunk), :].reshape(W, W)
    far_block = pick(far_block, jnp.transpose(far_block))
    block_high, block_low = halves(far_block)
    w.block_high[1] = block_high
    w.block_low[1] = block_low
    wide = dot(w.far_high[...], w.block_high[1]) + dot(w.far_high[...], w.block_low[1])
    wide = wide + dot(w.far_low[...], w.block_high[1]) + w.near_prod[...]
    out_ref[...] = 1.5 * band_ref[...] - wide * (0.5 / norm)


def kernel(s, names, wave_ref, ops_ref, map_ref, face_ref, out_ref, *scratch):
    w = types.SimpleNamespace(**dict(zip(names, scratch)))
    me = lax.axis_index("dom")
    barrier = pltpu.get_barrier_semaphore()
    greeted = [{"dom": lax.rem(me + 1, s.n_dom)}, {"dom": lax.rem(me + s.n_dom - 1, s.n_dom)}]
    if s.gram:
        chip, core = me // 2, lax.rem(me, 2)
        greeted.append({"dom": chip * 2 + (1 - core)})
        greeted.append({"band": 1 - lax.axis_index("band")})
        for j in range(1, s.chips):
            greeted.append({"dom": lax.rem(chip + j, s.chips) * 2 + core})
    for device in greeted:
        pl.semaphore_signal(barrier, inc=1, device_id=device, device_id_type=MESH)

    def ready():
        pl.semaphore_wait(barrier, len(greeted))

    if s.gram:
        if s.own_pad > s.own:
            w.bands[pl.ds(s.own, s.own_pad - s.own), :] = jnp.zeros((s.own_pad - s.own, s.width), f32)
        owned = w.bands.at[pl.ds(0, s.own), :]

        def send(q):
            band_copy(s, owned, w, 0, 1 - lax.axis_index("band"), q).start()

        filter_steps(s, ready, send, wave_ref, ops_ref, map_ref, face_ref, owned, w)
        gram_steps(s, owned, out_ref, w)
    else:
        filter_steps(s, ready, lambda q: None, wave_ref, ops_ref, map_ref, face_ref, out_ref, w)


def scratch_of(s):
    C, R, L, W, n, chunk = s.cells, s.rows, s.lanes, s.width, s.chips, s.chunk
    V, dma = pltpu.VMEM, pltpu.SemaphoreType.DMA
    scratch = dict(
        index=V((128, max(L, s.face_pad)), f32),
        face_rows=V((s.face, s.own_pad), bf16),
        vec=V((s.blocks, s.own_pad, 2 * s.block), bf16),
        take_own=V((C, R, s.own_pad), bf16),
        take_face=V((C, R, s.face_pad), bf16),
        put_own=V((s.own, C * L), bf16),
        put_face=V((s.face, C * L), bf16),
        put_back=V((s.own, s.face_pad), bf16),
        ops=V((s.nodes, C, s.nodes), f32),
        ops_sem=dma,
        op_pad=V((C, R, L), f32),
        op_high=V((C, R, L), bf16),
        op_low=V((C, R, L), bf16),
        part=V((s.blocks, C, R, 2 * s.block), f32),
        applied=V((s.blocks, s.own, s.block), f32),
        cell=V((C, L, 2 * s.block), bf16),
        prod=V((C * L, 2 * s.block), bf16),
        far=V((s.blocks, s.face_pad, 2 * s.block), bf16),
        latest=V((s.own, W), f32),
        older=V((s.own, W) if DEGREE > 2 else (8, 128), f32),
        face_send=V((DEGREE, s.blocks, s.face, s.block), f32),
        face_recv=V((DEGREE, s.blocks, s.face, s.block), f32),
        back_send=V((DEGREE, s.blocks, s.face, s.block), f32),
        back_recv=V((DEGREE, s.blocks, s.face, s.block), f32),
        face_ssem=dma((DEGREE, s.blocks)),
        face_rsem=dma((DEGREE, s.blocks)),
        back_ssem=dma((DEGREE, s.blocks)),
        back_rsem=dma((DEGREE, s.blocks)),
    )
    if s.gram:
        scratch |= dict(
            bands=V((s.own_pad, W), f32),
            far_band=V((s.own, W), f32),
            near_high=V((s.own_pad, W), bf16),
            near_low=V((s.own_pad, W), bf16),
            left_high=V((s.half_pad, W), bf16),
            left_low=V((s.half_pad, W), bf16),
            right_high=V((s.half_pad, W), bf16),
            right_low=V((s.half_pad, W), bf16),
            far_high=V((s.own, W), bf16),
            far_low=V((s.own, W), bf16),
            near_prod=V((s.own, W), f32),
            block_high=V((2, W, W), bf16),
            block_low=V((2, W, W), bf16),
            sums=V((2, 2, W // 2, W), f32),
            core_recv=V((2, W // 2, W), f32),
            pair=V((2, n, chunk, W), f32),
            scat_recv=V((2, n - 1, chunk, W), f32),
            full=V((2, 2, n, s.packet, W), f32),
            cross_send=V((s.packet, W), f32),
            cross_recv=V((s.packet, W), f32),
            cross_ssem=dma,
            cross_rsem=dma,
            band_ssem=dma((2, s.blocks)),
            band_rsem=dma((2, s.blocks)),
            core_ssem=dma((2,)),
            core_rsem=dma((2,)),
            swap_ssem=dma((2,)),
            swap_rsem=dma((2,)),
            scat_ssem=dma((2, n - 1)),
            scat_rsem=dma((2, n - 1)),
            gath_ssem=dma((2, n - 1)),
            gath_rsem=dma((2, n - 1)),
        )
    return scratch


def on_device(wavefun, cell_ops, cell_map, face_list):
    s = Sizes(lax.axis_size("dom"), lax.axis_size("band"), wavefun.shape[0], wavefun.shape[1],
              cell_map.shape[0], cell_map.shape[1], face_list.shape[0])
    scratch = scratch_of(s)
    latest = pl.pallas_call(
        functools.partial(kernel, s, list(scratch)),
        out_shape=jax.ShapeDtypeStruct(wavefun.shape, f32),
        in_specs=[pl.BlockSpec(memory_space=space) for space in (pltpu.VMEM, pl.ANY, pltpu.VMEM, pltpu.VMEM)],
        out_specs=pl.BlockSpec(memory_space=pltpu.VMEM),
        scratch_shapes=list(scratch.values()),
        compiler_params=pltpu.CompilerParams(
            collective_id=0, has_side_effects=True, vmem_limit_bytes=60 * 1024 * 1024),
        name="filtered_bands",
    )(wavefun, jnp.swapaxes(cell_ops, 0, 1), cell_map, face_list.reshape(1, -1))
    if s.gram:
        return latest
    full_bands = lax.all_gather(latest, "band", axis=1, tiled=True)
    partial_value = jnp.einsum("nb,nc->bc", full_bands, full_bands, precision=lax.Precision.HIGHEST)
    margin = lax.psum(partial_value, "dom")
    norm_value = jnp.sqrt(jnp.sum(margin * margin) + 1e-06)
    full_width = margin.shape[0]
    offset = lax.axis_index("band") * s.width
    scaled_cols = lax.dynamic_slice_in_dim(margin, offset, s.width, 1) / norm_value
    identity_cols = lax.dynamic_slice_in_dim(
        jnp.eye(full_width, dtype=jnp.float32), offset, s.width, 1
    )
    mixing = (3.0 * identity_cols - scaled_cols) / 2.0
    return jnp.dot(full_bands, mixing, precision=lax.Precision.HIGHEST)


def solution(mesh):
    return jax.shard_map(
        on_device,
        mesh=mesh,
        in_specs=(P("dom", "band"), P("dom", None, None), P("dom", None), P("dom")),
        out_specs=P("dom", "band"),
        check_vma=False,
    )
```
